512 devices in a mesh: sec: 64 (over x, z, core), op: 8 (over y).
Axes of the slice: x: 4, y: 8, z: 8, core: 2. Of those that a mesh axis runs over, the one named last changes fastest.
Arguments:
- wavefunction: bfloat16 [4096, 32, 384], P('sec'), may hold values from -6 to 6
- left_environment: bfloat16 [1024, 16, 32, 32], P('sec', 'op'), may hold values from -1 to 1
- right_environment: bfloat16 [128, 16, 384, 384], P('sec', 'op'), may hold values from -0.078125 to 0.078125
- left_table: int32 [4096, 3], P('sec'), may hold values from 0 to 63, as said below
- right_table: int32 [8192], P('sec'), may hold values from -1 to 1, as said below
Outputs:
- sigma: bfloat16 [4096, 32, 384], P('sec', None, 'op')
The draws below stay inside these ranges and needn't reach their ends.
Inputs may be any that keep to these rules, and one draw needn't show every extreme that they name: `left_table`: row g: column 0 is a left sector of the block's owner (below 16), column 1 the right owner along sec, column 2 a slot below 2; no two blocks of one left owner share columns 1 and 2; every left owner sends exactly 2 blocks to some right owner. `right_table`: entry p * 2 + c of right owner d's 128 entries is the right sector (below 2) of the block that left owner p sends to d in slot c, and -1 where p sends none there; it agrees with left_table.
All inputs are finite; a program needn't handle non-finite values.
Results may differ from the reference program's by a relative error of at most 0.017.
Values may be sent and summed in bfloat16 or wider, within the bound.
No kernel may reach another device: no remote copies, remote signals or barrier semaphores. Data moves between devices by JAX's collectives and lax.ppermute only.
A program may use at most 64 MiB of HBM per device.

```python
import jax
import jax.numpy as jnp
from jax import lax

BL = 32
BR = 384
NBD = 64
KG = 2
NSL = 16
NSR = 2
OWNERS = 64
GROUPS = 8
CAP = 2
SLOTS = 128
BLOCKS = 4096
KT = 16
LSECT = 1024
RSECT = 128


def build_tables(key):
    key_weight, key_raw, key_force, key_order, key_sector = jax.random.split(key, 5)
    shift_bits = jax.random.randint(key_weight, (OWNERS,), 0, 4)
    weight = jnp.left_shift(jnp.ones((OWNERS,), jnp.int32), shift_bits)
    raw_score = jax.random.randint(key_raw, (OWNERS, OWNERS, CAP), 0, 4096)
    slot_score = raw_score * weight[None, :, None]
    forced = jax.random.permutation(key_force, OWNERS)
    forced_hit = jnp.arange(OWNERS)[None, :] == forced[:, None]
    slot_score = jnp.where(forced_hit[:, :, None], 65536, slot_score)
    ranked = slot_score.reshape(OWNERS, SLOTS) * SLOTS + jnp.arange(SLOTS, dtype=jnp.int32)[None, :]
    top_values, chosen = lax.top_k(ranked, NBD)
    shuffle = jax.random.randint(key_order, (OWNERS, NBD), 0, 4096) * NBD + jnp.arange(NBD, dtype=jnp.int32)[None, :]
    new_order = jnp.argsort(shuffle, axis=1)
    chosen = jnp.take_along_axis(chosen, new_order, axis=1).astype(jnp.int32)
    left_sector = jax.random.randint(key_sector, (OWNERS, NBD), 0, NSL)
    right_sector = jax.random.randint(jax.random.fold_in(key_sector, 1), (OWNERS, NBD), 0, NSR)
    left_rows = jnp.stack([left_sector, chosen // CAP, chosen % CAP], axis=-1).reshape(BLOCKS, 3)
    by_sender = jnp.full((OWNERS, SLOTS), -1, jnp.int32).at[jnp.arange(OWNERS)[:, None], chosen].set(right_sector)
    right_rows = by_sender.reshape(OWNERS, OWNERS, CAP).transpose(1, 0, 2).reshape(OWNERS * SLOTS)
    return (left_rows.astype(jnp.int32), right_rows.astype(jnp.int32))


def draw_left_table(key, part):
    return build_tables(jax.random.fold_in(key, 11))[0]


def draw_right_table(key, part):
    return build_tables(jax.random.fold_in(key, 11))[1]


def block_scale(own_key, shape, cuts, smallest, top_value):
    def one(axis_at, blocks):
        heights = jax.random.uniform(jax.random.fold_in(jax.random.fold_in(own_key, 6), axis_at), (blocks,), jnp.float32, smallest / len(cuts), top_value / len(cuts))
        return jnp.repeat(jnp.exp(heights), shape[axis_at] // blocks).reshape((-1,) + (1,) * (len(shape) - axis_at - 1))

    factor_of = one(*cuts[0])
    for cut in cuts[1:]:
        factor_of = factor_of * one(*cut)
    return factor_of


def gaussian(rng, extent, deviation, bound, cuts=(), kind=jnp.bfloat16):
    values = jax.random.normal(rng, extent, jnp.float32) * deviation
    if len(cuts) > 0:
        values = block_scale(rng, extent, cuts, -0.22, 0.18) * values
    return jnp.clip(values, min=-bound, max=bound).astype(kind)


def setup_inputs(seed: int = 0) -> dict:
    streams_of = jax.random.split(jax.random.key(seed), 6)
    wavefunction = gaussian(streams_of[0], (BLOCKS, BL, BR), 1.0, 6.0, ((0, 64),))
    left_environment = gaussian(streams_of[1], (LSECT, KT, BL, BL), BL ** -0.5, 1.0, ((0, 64), (1, 8)))
    right_environment = gaussian(streams_of[2], (RSECT, KT, BR, BR), (BR * KT) ** -0.5, 0.078125, ((0, 64), (1, 8)))
    left_table = draw_left_table(jax.random.fold_in(streams_of[5], 71), 0)
    right_table = draw_right_table(jax.random.fold_in(streams_of[5], 71), 0)
    return {"wavefunction": wavefunction, "left_environment": left_environment, "right_environment": right_environment, "left_table": left_table, "right_table": right_table}


def block_sectors(left_table, right_table):
    owner_left = jnp.arange(BLOCKS, dtype=jnp.int32) // NBD
    left_sector = (owner_left * NSL + left_table[:, 0]).astype(jnp.int32)
    right_owner = left_table[:, 1]
    table_entry = right_table[(right_owner * SLOTS + owner_left * CAP + left_table[:, 2]).astype(jnp.int32)]
    live_block = (table_entry >= 0).astype(jnp.float32)
    right_sector = (right_owner * NSR + jnp.maximum(table_entry, 0)).astype(jnp.int32)
    return left_sector, right_sector, live_block


def reference(wavefunction, left_environment, right_environment, left_table, right_table):
    left_sector, right_sector, live_block = block_sectors(left_table, right_table)

    def one_block(members):
        block_data, left_index, right_index, is_live = members
        left_mats = left_environment[left_index].astype(jnp.float32)
        right_mats = right_environment[right_index].astype(jnp.float32)
        products = jnp.einsum("kab,bc->kac", left_mats, block_data.astype(jnp.float32))
        products = lax.optimization_barrier(products.astype(jnp.bfloat16)).astype(jnp.float32)
        grouped = jnp.einsum("oiab,oibc->oac", products.reshape(GROUPS, KG, BL, BR), right_mats.reshape(GROUPS, KG, BR, BR))
        partial_value = lax.optimization_barrier((grouped * is_live).astype(jnp.bfloat16)).astype(jnp.float32)
        return jnp.sum(partial_value, axis=0).astype(jnp.bfloat16)

    return lax.map(one_block, (wavefunction, left_sector, right_sector, live_block))
```

```python
import functools

import jax
import jax.numpy as jnp
from jax import lax
from jax.experimental import pallas as pl
from jax.experimental.pallas import tpu as pltpu
from jax.sharding import PartitionSpec as P

BF16 = jnp.bfloat16
F32 = jnp.float32


def iota(shape, dim):
    return lax.broadcasted_iota(jnp.int32, shape, dim)


def contract_kernel(sector_ref, psi_ref, left_ref, *rest):
    right_refs, (out_ref, right_scr, x_scr, part_scr, piece_scr, sem) = rest[:7], rest[7:]
    copies = []
    for term in range(8):
        for sector in range(2):
            source = right_refs[0].at[sector, term] if term < 2 else right_refs[term - 1].at[sector]
            copies.append(
                pltpu.make_async_copy(
                    source,
                    right_scr.at[pl.ds(term * 384, 384), pl.ds(sector * 384, 384)],
                    sem.at[term * 2 + sector],
                )
            )
    for copy in copies:
        copy.start()

    lane, column = iota((128, 256), 0), iota((128, 256), 1)
    spread = [
        jnp.where(((lane >> 5) == kk) & ((lane & 31) == (column & 31)), 1.0, 0.0).astype(BF16)
        for kk in range(4)
    ]
    same_block = (iota((256, 256), 0) >> 5) == (iota((256, 256), 1) >> 5)

    def left_group(index, carry):
        left = left_ref[pl.ds(index * 8, 8)].reshape(256, 128)
        psi = psi_ref[pl.ds(index * 8, 8)].reshape(256, 384)
        row = pl.multiple_of(index * 128, 128)
        for kk in range(4):
            wide = jnp.dot(left, spread[kk], preferred_element_type=F32)
            wide = jnp.where(same_block, wide, 0.0).astype(BF16)
            product = jnp.dot(wide, psi, preferred_element_type=F32).astype(BF16)
            product = product.reshape(8, 2, 16, 384)
            for half in range(2):
                term = half * 4 + kk
                x_scr[pl.ds(row, 128), term * 384 : term * 384 + 384] = product[:, half].reshape(128, 384)
        return carry

    lax.fori_loop(0, 8, left_group, 0)
    for copy in copies:
        copy.wait()

    place = iota((384, 384), 1)
    wanted = 48 * ((place >> 4) & 7) + 16 * (place >> 7) + (place & 15)
    reorder = jnp.where(iota((384, 384), 0) == wanted, 1.0, 0.0).astype(BF16)

    def right_group(index, carry):
        row = pl.multiple_of(index * 256, 256)
        total = jnp.dot(x_scr[pl.ds(row, 256), :], right_scr[...], preferred_element_type=F32)
        chosen = []
        for j in range(16):
            entry = sector_ref[index * 16 + j]
            rows = total[j * 16 : j * 16 + 16]
            rows = jnp.where(entry == 1, rows[:, 384:], rows[:, :384])
            chosen.append(jnp.where(entry >= 0, rows, 0.0))
        chosen = jnp.concatenate(chosen, axis=0).astype(BF16)
        ordered = jnp.dot(chosen, reorder, preferred_element_type=F32)
        for tile in range(3):
            part_scr[pl.ds(tile * 1024 + row, 256), :] = ordered[:, tile * 128 : tile * 128 + 128]
        return carry

    lax.fori_loop(0, 4, right_group, 0)

    lane_group = iota((64, 128), 1) >> 4
    for upper in range(2):
        for tile in range(3):
            rows = [
                part_scr[pl.ds(tile * 1024 + upper * 8 + a, 64, stride=16), :]
                for a in range(8)
            ]
            for bit in range(3):
                low_lane = ((lane_group >> bit) & 1) == 0
                shift = 16 << bit
                for a in range(8):
                    if a & (1 << bit):
                        continue
                    first, second = rows[a], rows[a | (1 << bit)]
                    rows[a] = jnp.where(low_lane, first, pltpu.roll(second, shift, 1))
                    rows[a | (1 << bit)] = jnp.where(low_lane, pltpu.roll(first, 128 - shift, 1), second)
            for target in range(8):
                piece_scr[pl.ds(target * 6 + upper * 3 + tile, 64, stride=48), :] = rows[target]
    out_ref[...] = piece_scr[...].astype(BF16)


def contract(slot_sector, psi, left, rights):
    vmem = pl.BlockSpec(memory_space=pltpu.VMEM)
    return pl.pallas_call(
        contract_kernel,
        out_shape=jax.ShapeDtypeStruct((3072, 128), BF16),
        in_specs=[pl.BlockSpec(memory_space=pltpu.SMEM), vmem, vmem]
        + [pl.BlockSpec(memory_space=pl.ANY)] * 7,
        out_specs=vmem,
        scratch_shapes=[
            pltpu.VMEM((3072, 768), BF16),
            pltpu.VMEM((1024, 3072), BF16),
            pltpu.VMEM((3072, 128), F32),
            pltpu.VMEM((3072, 128), F32),
            pltpu.SemaphoreType.DMA((16,)),
        ],
        compiler_params=pltpu.CompilerParams(vmem_limit_bytes=40 << 20),
        cost_estimate=pl.CostEstimate(flops=7_000_000_000, bytes_accessed=8_000_000, transcendentals=0),
        name="contract",
    )(slot_sector, psi, left, *rights)


def collect_kernel(table_ref, piece_ref, out_ref, wide_scr):
    wide_scr[...] = piece_ref[...].astype(F32)
    slot = iota((64, 256), 1)
    owner = table_ref[:, 1:2]
    place = table_ref[:, 2:3]
    pick = jnp.where(((slot >> 2) == owner) & ((slot & 1) == place), 1.0, 0.0).astype(BF16)
    for half in range(2):
        for upper in range(2):
            for tile in range(3):
                rows = wide_scr[pl.ds(half * 6 + upper * 3 + tile, 256, stride=12), :].astype(BF16)
                total = jnp.dot(pick, rows, preferred_element_type=F32)
                first = half * 16 + upper * 8
                out_ref[first : first + 8, tile * 16 : tile * 16 + 16, :] = (
                    total.T.reshape(8, 16, 64).astype(BF16)
                )


def collect(left_table, pieces):
    vmem = pl.BlockSpec(memory_space=pltpu.VMEM)
    return pl.pallas_call(
        collect_kernel,
        out_shape=jax.ShapeDtypeStruct((32, 48, 64), BF16),
        in_specs=[vmem, vmem],
        out_specs=vmem,
        scratch_shapes=[pltpu.VMEM((3072, 128), F32)],
        name="collect",
    )(left_table, pieces)


def per_device(psi, left, right, left_table, right_table):
    me = lax.axis_index("op")
    slot, half = (me >> 1) & 1, me & 1
    hop = lambda value, step: lax.ppermute(value, "op", [(i, (i + step) % 8) for i in range(8)])

    match = (left_table[:, 1:2] == jnp.arange(64)[None, :]) & (left_table[:, 2:3] == slot)
    source = jnp.sum(jnp.where(match, jnp.arange(64)[:, None], 0), axis=0)
    left_of = jnp.sum(jnp.where(match, left_table[:, :1], 0), axis=0)
    psi_there = lax.all_to_all(
        psi.at[source].get(mode="promise_in_bounds"), "sec", split_axis=0, concat_axis=0, tiled=True
    )

    dense = left.reshape(16, 2, 2, 16, 32).transpose(0, 3, 2, 1, 4).reshape(16, 16, 128)
    before, after = hop(dense, 1), hop(dense, -1)
    two_before, two_after = hop(dense, 2), hop(dense, -2)
    part = lambda value: jnp.where(half == 0, value[:, :, :64], value[:, :, 64:])
    table = jnp.concatenate(
        [
            jnp.concatenate([part(dense), part(before)], axis=2),
            jnp.concatenate([part(after), part(two_before)[:, :, 32:], part(two_after)[:, :, :32]], axis=2),
        ],
        axis=1,
    )
    first, second = right[:, 0], right[:, 1]
    left_here, psi_there, before_second, after_first, before_first, after_second = lax.optimization_barrier(
        (
            table.at[left_of].get(mode="promise_in_bounds"),
            psi_there,
            hop(second, 1),
            hop(first, -1),
            hop(first, 1),
            hop(second, -1),
        )
    )
    left_there = lax.all_to_all(left_here, "sec", split_axis=0, concat_axis=0, tiled=True)
    two_before_second, two_after_first = hop(before_second, 1), hop(after_first, -1)

    slot_sector = jnp.where(slot == 0, right_table.reshape(64, 2)[:, 0], right_table.reshape(64, 2)[:, 1])
    pieces = contract(
        slot_sector,
        psi_there,
        left_there,
        [right, before_first, before_second, after_first, after_second, two_before_second, two_after_first],
    )
    pieces = lax.all_to_all(
        pieces.reshape(512, 3, 2, 128), ("sec", "op"), split_axis=0, concat_axis=0, tiled=True
    )
    return collect(left_table, pieces.reshape(3072, 128)).transpose(2, 0, 1)


def solution(mesh):
    in_specs = (
        P("sec", None, None),
        P("sec", "op", None, None),
        P("sec", "op", None, None),
        P("sec", None),
        P("sec"),
    )
    out_specs = P("sec", None, "op")
    return jax.shard_map(
        per_device, mesh=mesh, in_specs=in_specs, out_specs=out_specs, check_vma=False
    )
```

```python
import functools

import jax
import jax.numpy as jnp
from jax import lax
from jax.experimental import pallas as pl
from jax.experimental.pallas import tpu as pltpu
from jax.sharding import PartitionSpec as P

BF16 = jnp.bfloat16
F32 = jnp.float32


def iota(shape, dim):
    return lax.broadcasted_iota(jnp.int32, shape, dim)


def contract_kernel(sector_ref, psi_ref, left_ref, *rest):
    right_refs, (out_ref, right_scr, x_scr, part_scr, piece_scr, sem) = rest[:5], rest[5:]
    copies = []
    for term in range(8):
        for sector in range(2):
            if term < 2:
                source = right_refs[0].at[sector, term]
            elif term < 6:
                source = right_refs[term // 2].at[term % 2, sector]
            else:
                source = right_refs[term - 3].at[sector]
            copies.append(
                pltpu.make_async_copy(
                    source,
                    right_scr.at[pl.ds(term * 384, 384), pl.ds(sector * 384, 384)],
                    sem.at[term * 2 + sector],
                )
            )
    for copy in copies:
        copy.start()

    lane, column = iota((128, 1024), 0), iota((128, 1024), 1)
    spread = jnp.where(
        ((lane >> 5) == (column >> 8)) & ((lane & 31) == (column & 31)), 1.0, 0.0
    ).astype(BF16)
    same_block = (iota((256, 256), 0) >> 5) == (iota((256, 256), 1) >> 5)

    def left_group(index, carry):
        left = left_ref[pl.ds(index * 8, 8)].reshape(256, 128)
        psi = psi_ref[pl.ds(index * 8, 8)].reshape(256, 384)
        row = pl.multiple_of(index * 128, 128)
        wide = jnp.dot(left, spread, preferred_element_type=F32)
        wide = jnp.concatenate(
            [jnp.where(same_block, wide[:, kk * 256 : kk * 256 + 256], 0.0).astype(BF16) for kk in range(4)],
            axis=0,
        )
        product = jnp.dot(wide, psi, preferred_element_type=F32).astype(BF16).reshape(4, 8, 2, 16, 384)
        for kk in range(4):
            for half in range(2):
                term = half * 4 + kk
                x_scr[pl.ds(row, 128), term * 384 : term * 384 + 384] = product[kk, :, half].reshape(128, 384)
        return carry

    lax.fori_loop(0, 8, left_group, 0, unroll=2)
    for copy in copies:
        copy.wait()

    place = iota((384, 384), 1)
    wanted = 48 * ((place >> 4) & 7) + 16 * (place >> 7) + (place & 15)
    reorder = jnp.where(iota((384, 384), 0) == wanted, 1.0, 0.0).astype(BF16)

    def right_group(index, carry):
        row = pl.multiple_of(index * 1024, 1024)
        total = jnp.dot(x_scr[pl.ds(row, 1024), :], right_scr[...], preferred_element_type=F32)
        chosen = []
        for j in range(64):
            entry = sector_ref[index * 64 + j]
            rows = total[j * 16 : j * 16 + 16]
            rows = jnp.where(entry == 1, rows[:, 384:], rows[:, :384])
            chosen.append(jnp.where(entry >= 0, rows, 0.0))
        chosen = jnp.concatenate(chosen, axis=0).astype(BF16)
        ordered = jnp.dot(chosen, reorder, preferred_element_type=F32)
        for tile in range(3):
            part_scr[pl.ds(tile * 1024 + row, 1024), :] = ordered[:, tile * 128 : tile * 128 + 128]
        return carry

    lax.fori_loop(0, 1, right_group, 0)

    lane_group = iota((64, 128), 1) >> 4
    for upper in range(2):
        for tile in range(3):
            rows = [
                part_scr[pl.ds(tile * 1024 + upper * 8 + a, 64, stride=16), :]
                for a in range(8)
            ]
            for bit in range(3):
                low_lane = ((lane_group >> bit) & 1) == 0
                shift = 16 << bit
                for a in range(8):
                    if a & (1 << bit):
                        continue
                    first, second = rows[a], rows[a | (1 << bit)]
                    rows[a] = jnp.where(low_lane, first, pltpu.roll(second, shift, 1))
                    rows[a | (1 << bit)] = jnp.where(low_lane, pltpu.roll(first, 128 - shift, 1), second)
            for target in range(8):
                piece_scr[pl.ds(target * 6 + upper * 3 + tile, 64, stride=48), :] = rows[target]
    out_ref[...] = piece_scr[...].astype(BF16)


def contract(slot_sector, psi, left, rights):
    vmem = pl.BlockSpec(memory_space=pltpu.VMEM)
    return pl.pallas_call(
        contract_kernel,
        out_shape=jax.ShapeDtypeStruct((3072, 128), BF16),
        in_specs=[pl.BlockSpec(memory_space=pltpu.SMEM), vmem, vmem]
        + [pl.BlockSpec(memory_space=pltpu.HBM)] * 5,
        out_specs=vmem,
        scratch_shapes=[
            pltpu.VMEM((3072, 768), BF16),
            pltpu.VMEM((1024, 3072), BF16),
            pltpu.VMEM((3072, 128), F32),
            pltpu.VMEM((3072, 128), F32),
            pltpu.SemaphoreType.DMA((16,)),
        ],
        compiler_params=pltpu.CompilerParams(vmem_limit_bytes=60 << 20),
        cost_estimate=pl.CostEstimate(flops=7_000_000_000, bytes_accessed=8_000_000, transcendentals=0),
        name="contract",
    )(slot_sector, psi, left, *rights)


def collect_kernel(table_ref, piece_ref, out_ref, wide_scr):
    wide_scr[...] = piece_ref[...].astype(F32)
    slot = iota((64, 256), 1)
    owner = table_ref[:, 1:2]
    place = table_ref[:, 2:3]
    pick = jnp.where(((slot >> 2) == owner) & ((slot & 1) == place), 1.0, 0.0).astype(BF16)
    for half in range(2):
        for upper in range(2):
            for tile in range(3):
                rows = wide_scr[pl.ds(half * 6 + upper * 3 + tile, 256, stride=12), :].astype(BF16)
                total = jnp.dot(pick, rows, preferred_element_type=F32)
                first = half * 16 + upper * 8
                out_ref[first : first + 8, tile * 16 : tile * 16 + 16, :] = (
                    total.T.reshape(8, 16, 64).astype(BF16)
                )


def collect(left_table, pieces):
    vmem = pl.BlockSpec(memory_space=pltpu.VMEM)
    return pl.pallas_call(
        collect_kernel,
        out_shape=jax.ShapeDtypeStruct((32, 48, 64), BF16),
        in_specs=[vmem, vmem],
        out_specs=vmem,
        scratch_shapes=[pltpu.VMEM((3072, 128), F32)],
        compiler_params=pltpu.CompilerParams(vmem_limit_bytes=60 << 20),
        name="collect",
    )(left_table, pieces)


def per_device(psi, left, right, left_table, right_table):
    me = lax.axis_index("op")
    slot, half = (me >> 1) & 1, me & 1
    hop = lambda value, step: lax.ppermute(value, "op", [(i, (i + step) % 8) for i in range(8)])

    match = (left_table[:, 1:2] == jnp.arange(64)[None, :]) & (left_table[:, 2:3] == slot)
    source = jnp.sum(jnp.where(match, jnp.arange(64)[:, None], 0), axis=0)
    left_of = jnp.sum(jnp.where(match, left_table[:, :1], 0), axis=0)
    psi_there = lax.all_to_all(
        psi.at[source].get(mode="promise_in_bounds"), "sec", split_axis=0, concat_axis=0, tiled=True
    )

    dense = left.reshape(16, 2, 2, 16, 32).transpose(0, 3, 2, 1, 4).reshape(16, 16, 128)
    by_term = right.transpose(1, 0, 2, 3)
    before, after, two_before, two_after, right_before, right_after = lax.optimization_barrier(
        (hop(dense, 1), hop(dense, -1), hop(dense, 2), hop(dense, -2), hop(by_term, 1), hop(by_term, -1))
    )
    part = lambda value: jnp.where(half == 0, value[:, :, :64], value[:, :, 64:])
    table = jnp.concatenate(
        [
            jnp.concatenate([part(dense), part(before)], axis=2),
            jnp.concatenate([part(after), part(two_before)[:, :, 32:], part(two_after)[:, :, :32]], axis=2),
        ],
        axis=1,
    )
    left_here, psi_there = lax.optimization_barrier(
        (table.at[left_of].get(mode="promise_in_bounds"), psi_there)
    )
    left_there = lax.all_to_all(left_here, "sec", split_axis=0, concat_axis=0, tiled=True)
    right_two_before, right_two_after = hop(right_before[1], 1), hop(right_after[0], -1)

    slot_sector = jnp.where(slot == 0, right_table.reshape(64, 2)[:, 0], right_table.reshape(64, 2)[:, 1])
    pieces = contract(
        slot_sector,
        psi_there,
        left_there,
        [right, right_before, right_after, right_two_before, right_two_after],
    )
    pieces = lax.all_to_all(
        pieces.reshape(512, 3, 2, 128), ("sec", "op"), split_axis=0, concat_axis=0, tiled=True
    )
    return collect(left_table, pieces.reshape(3072, 128)).transpose(2, 0, 1)


def solution(mesh):
    in_specs = (
        P("sec", None, None),
        P("sec", "op", None, None),
        P("sec", "op", None, None),
        P("sec", None),
        P("sec"),
    )
    out_specs = P("sec", None, "op")
    return jax.shard_map(
        per_device, mesh=mesh, in_specs=in_specs, out_specs=out_specs, check_vma=False
    )
```

```python
import functools

import jax
import jax.numpy as jnp
from jax import lax
from jax.experimental import pallas as pl
from jax.experimental.pallas import tpu as pltpu
from jax.sharding import PartitionSpec as P

BF16 = jnp.bfloat16
F32 = jnp.float32


def iota(shape, dim):
    return lax.broadcasted_iota(jnp.int32, shape, dim)


def contract_kernel(sector_ref, psi_ref, left_ref, *rest):
    right_refs, (out_ref, right_scr, x_scr, part_scr, piece_scr, sem) = rest[:5], rest[5:]
    copies = []
    for term in range(8):
        for sector in range(2):
            if term < 6:
                source = right_refs[term // 2].at[sector, term % 2]
            else:
                source = right_refs[term - 3].at[sector]
            copies.append(
                pltpu.make_async_copy(
                    source,
                    right_scr.at[pl.ds(term * 384, 384), pl.ds(sector * 384, 384)],
                    sem.at[term * 2 + sector],
                )
            )
    for copy in copies:
        copy.start()

    lane, column = iota((128, 1024), 0), iota((128, 1024), 1)
    spread = jnp.where(
        ((lane >> 5) == (column >> 8)) & ((lane & 31) == (column & 31)), 1.0, 0.0
    ).astype(BF16)
    same_block = (iota((256, 256), 0) >> 5) == (iota((256, 256), 1) >> 5)

    def left_group(index, carry):
        left = left_ref[pl.ds(index * 8, 8)].reshape(256, 128)
        psi = psi_ref[pl.ds(index * 8, 8)].reshape(256, 384)
        row = pl.multiple_of(index * 128, 128)
        wide = jnp.dot(left, spread, preferred_element_type=F32)
        wide = jnp.concatenate(
            [jnp.where(same_block, wide[:, kk * 256 : kk * 256 + 256], 0.0).astype(BF16) for kk in range(4)],
            axis=0,
        )
        product = jnp.dot(wide, psi, preferred_element_type=F32).astype(BF16).reshape(4, 8, 2, 16, 384)
        for kk in range(4):
            for half in range(2):
                term = half * 4 + kk
                x_scr[pl.ds(row, 128), term * 384 : term * 384 + 384] = product[kk, :, half].reshape(128, 384)
        return carry

    lax.fori_loop(0, 8, left_group, 0, unroll=2)
    for copy in copies:
        copy.wait()

    place = iota((384, 384), 1)
    wanted = 48 * ((place >> 4) & 7) + 16 * (place >> 7) + (place & 15)
    reorder = jnp.where(iota((384, 384), 0) == wanted, 1.0, 0.0).astype(BF16)

    def right_group(index, carry):
        row = pl.multiple_of(index * 1024, 1024)
        total = jnp.dot(x_scr[pl.ds(row, 1024), :], right_scr[...], preferred_element_type=F32)
        chosen = []
        for j in range(64):
            entry = sector_ref[index * 64 + j]
            rows = total[j * 16 : j * 16 + 16]
            rows = jnp.where(entry == 1, rows[:, 384:], rows[:, :384])
            chosen.append(jnp.where(entry >= 0, rows, 0.0))
        chosen = jnp.concatenate(chosen, axis=0).astype(BF16)
        ordered = jnp.dot(chosen, reorder, preferred_element_type=F32)
        for tile in range(3):
            part_scr[pl.ds(tile * 1024 + row, 1024), :] = ordered[:, tile * 128 : tile * 128 + 128]
        return carry

    lax.fori_loop(0, 1, right_group, 0)

    lane_group = iota((64, 128), 1) >> 4
    for upper in range(2):
        for tile in range(3):
            rows = [
                part_scr[pl.ds(tile * 1024 + upper * 8 + a, 64, stride=16), :]
                for a in range(8)
            ]
            for bit in range(3):
                low_lane = ((lane_group >> bit) & 1) == 0
                shift = 16 << bit
                for a in range(8):
                    if a & (1 << bit):
                        continue
                    first, second = rows[a], rows[a | (1 << bit)]
                    rows[a] = jnp.where(low_lane, first, pltpu.roll(second, shift, 1))
                    rows[a | (1 << bit)] = jnp.where(low_lane, pltpu.roll(first, 128 - shift, 1), second)
            for target in range(8):
                piece_scr[pl.ds(target * 6 + upper * 3 + tile, 64, stride=48), :] = rows[target]
    out_ref[...] = piece_scr[...].astype(BF16)


def contract(slot_sector, psi, left, rights):
    vmem = pl.BlockSpec(memory_space=pltpu.VMEM)
    return pl.pallas_call(
        contract_kernel,
        out_shape=jax.ShapeDtypeStruct((3072, 128), BF16),
        in_specs=[pl.BlockSpec(memory_space=pltpu.SMEM), vmem, vmem]
        + [pl.BlockSpec(memory_space=pltpu.HBM)] * 5,
        out_specs=vmem,
        scratch_shapes=[
            pltpu.VMEM((3072, 768), BF16),
            pltpu.VMEM((1024, 3072), BF16),
            pltpu.VMEM((3072, 128), F32),
            pltpu.VMEM((3072, 128), F32),
            pltpu.SemaphoreType.DMA((16,)),
        ],
        compiler_params=pltpu.CompilerParams(vmem_limit_bytes=60 << 20),
        cost_estimate=pl.CostEstimate(flops=7_000_000_000, bytes_accessed=8_000_000, transcendentals=0),
        name="contract",
    )(slot_sector, psi, left, *rights)


def collect_kernel(table_ref, piece_ref, out_ref, wide_scr):
    wide_scr[...] = piece_ref[...].astype(F32)
    slot = iota((256, 64), 0)
    chosen = ((slot >> 2) == table_ref[1:2]) & ((slot & 1) == table_ref[2:3])
    wanted = jnp.where(chosen, 1.0, 0.0).T.astype(BF16)
    for half in range(2):
        for upper in range(2):
            for tile in range(3):
                rows = wide_scr[pl.ds(half * 6 + upper * 3 + tile, 256, stride=12), :].astype(BF16)
                total = jnp.dot(wanted, rows, preferred_element_type=F32)
                first = half * 16 + upper * 8
                out_ref[first : first + 8, tile * 16 : tile * 16 + 16, :] = (
                    total.T.reshape(8, 16, 64).astype(BF16)
                )


def collect(left_table, pieces):
    vmem = pl.BlockSpec(memory_space=pltpu.VMEM)
    return pl.pallas_call(
        collect_kernel,
        out_shape=jax.ShapeDtypeStruct((32, 48, 64), BF16),
        in_specs=[vmem, vmem],
        out_specs=vmem,
        scratch_shapes=[pltpu.VMEM((3072, 128), F32)],
        compiler_params=pltpu.CompilerParams(vmem_limit_bytes=16 << 20),
        name="collect",
    )(left_table, pieces)


def pick_kernel(term, right_ref, out_ref, sem):
    copies = [
        pltpu.make_async_copy(right_ref.at[sector, term], out_ref.at[sector], sem.at[sector]) for sector in range(2)
    ]
    for copy in copies:
        copy.start()
    for copy in copies:
        copy.wait()


def pick(right, term):
    return pl.pallas_call(
        functools.partial(pick_kernel, term),
        out_shape=jax.ShapeDtypeStruct((2, 384, 384), BF16),
        in_specs=[pl.BlockSpec(memory_space=pltpu.HBM)],
        out_specs=pl.BlockSpec(memory_space=pltpu.HBM),
        scratch_shapes=[pltpu.SemaphoreType.DMA((2,))],
        compiler_params=pltpu.CompilerParams(vmem_limit_bytes=60 << 20),
        name="pick",
    )(right)


def per_device(psi, left, right, left_table, right_table):
    me = lax.axis_index("op")
    slot, half = (me >> 1) & 1, me & 1
    hop = lambda value, step: lax.ppermute(value, "op", [(i, (i + step) % 8) for i in range(8)])

    match = (left_table[:, 1:2] == jnp.arange(64)[None, :]) & (left_table[:, 2:3] == slot)
    source = jnp.sum(jnp.where(match, jnp.arange(64)[:, None], 0), axis=0)
    left_of = jnp.sum(jnp.where(match, left_table[:, :1], 0), axis=0)
    psi_there = lax.all_to_all(
        psi.at[source].get(mode="promise_in_bounds"), "sec", split_axis=0, concat_axis=0, tiled=True
    )

    dense = left.reshape(16, 2, 2, 16, 32).transpose(0, 3, 2, 1, 4).reshape(16, 16, 128)
    before, after, two_before, two_after = hop(dense, 1), hop(dense, -1), hop(dense, 2), hop(dense, -2)
    right_before, right_after = hop(right, 1), hop(right, -1)
    part = lambda value: jnp.where(half == 0, value[:, :, :64], value[:, :, 64:])
    table = jnp.concatenate(
        [
            jnp.concatenate([part(dense), part(before)], axis=2),
            jnp.concatenate([part(after), part(two_before)[:, :, 32:], part(two_after)[:, :, :32]], axis=2),
        ],
        axis=1,
    )
    left_here, psi_there = lax.optimization_barrier(
        (table.at[left_of].get(mode="promise_in_bounds"), psi_there)
    )
    left_there = lax.all_to_all(left_here, "sec", split_axis=0, concat_axis=0, tiled=True)
    right_two_before, right_two_after = hop(pick(right_before, 1), 1), hop(pick(right_after, 0), -1)

    slot_sector = jnp.where(slot == 0, right_table.reshape(64, 2)[:, 0], right_table.reshape(64, 2)[:, 1])
    pieces = contract(
        slot_sector,
        psi_there,
        left_there,
        [right, right_before, right_after, right_two_before, right_two_after],
    )
    pieces = lax.all_to_all(
        pieces.reshape(512, 3, 2, 128), ("sec", "op"), split_axis=0, concat_axis=0, tiled=True
    )
    return collect(left_table.T, pieces.reshape(3072, 128)).transpose(2, 0, 1)


def solution(mesh):
    in_specs = (
        P("sec", None, None),
        P("sec", "op", None, None),
        P("sec", "op", None, None),
        P("sec", None),
        P("sec"),
    )
    out_specs = P("sec", None, "op")
    return jax.shard_map(
        per_device, mesh=mesh, in_specs=in_specs, out_specs=out_specs, check_vma=False
    )
```

```python
import jax
import jax.numpy as jnp
from jax import lax
from jax.experimental import pallas as pl
from jax.experimental.pallas import tpu as pltpu
from jax.sharding import PartitionSpec as P

BF16 = jnp.bfloat16
F32 = jnp.float32


def iota(shape, dim):
    return lax.broadcasted_iota(jnp.int32, shape, dim)


def contract_kernel(sector_ref, psi_ref, left_ref, *rest):
    right_refs, (out_ref, right_scr, x_scr, part_scr, piece_scr, sem) = rest[:5], rest[5:]
    copies = []
    for term in range(8):
        for sector in range(2):
            if term < 6:
                source = right_refs[term // 2].at[sector, term % 2]
            else:
                source = right_refs[term - 3].at[sector]
            copies.append(
                pltpu.make_async_copy(
                    source,
                    right_scr.at[pl.ds(term * 384, 384), pl.ds(sector * 384, 384)],
                    sem.at[term * 2 + sector],
                )
            )
    for copy in copies:
        copy.start()

    lane, column = iota((128, 1024), 0), iota((128, 1024), 1)
    spread = jnp.where(
        ((lane >> 5) == (column >> 8)) & ((lane & 31) == (column & 31)), 1.0, 0.0
    ).astype(BF16)
    same_block = (iota((256, 256), 0) >> 5) == (iota((256, 256), 1) >> 5)

    def left_group(index, carry):
        left = left_ref[pl.ds(index * 8, 8)].reshape(256, 128)
        psi = psi_ref[pl.ds(index * 8, 8)].reshape(256, 384)
        row = pl.multiple_of(index * 128, 128)
        wide = jnp.dot(left, spread, preferred_element_type=F32)
        wide = jnp.concatenate(
            [jnp.where(same_block, wide[:, kk * 256 : kk * 256 + 256], 0.0).astype(BF16) for kk in range(4)],
            axis=0,
        )
        product = jnp.dot(wide, psi, preferred_element_type=F32).astype(BF16).reshape(4, 8, 2, 16, 384)
        for kk in range(4):
            for half in range(2):
                term = half * 4 + kk
                x_scr[pl.ds(row, 128), term * 384 : term * 384 + 384] = product[kk, :, half].reshape(128, 384)
        return carry

    lax.fori_loop(0, 8, left_group, 0, unroll=2)
    for copy in copies:
        copy.wait()

    place = iota((384, 384), 1)
    wanted = 48 * ((place >> 4) & 7) + 16 * (place >> 7) + (place & 15)
    reorder = jnp.where(iota((384, 384), 0) == wanted, 1.0, 0.0).astype(BF16)

    def right_group(index, carry):
        row = pl.multiple_of(index * 1024, 1024)
        total = jnp.dot(x_scr[pl.ds(row, 1024), :], right_scr[...], preferred_element_type=F32)
        chosen = []
        for j in range(64):
            entry = sector_ref[index * 64 + j]
            rows = total[j * 16 : j * 16 + 16]
            rows = jnp.where(entry == 1, rows[:, 384:], rows[:, :384])
            chosen.append(jnp.where(entry >= 0, rows, 0.0))
        chosen = jnp.concatenate(chosen, axis=0).astype(BF16)
        ordered = jnp.dot(chosen, reorder, preferred_element_type=F32)
        for tile in range(3):
            part_scr[pl.ds(tile * 1024 + row, 1024), :] = ordered[:, tile * 128 : tile * 128 + 128]
        return carry

    lax.fori_loop(0, 1, right_group, 0)

    lane_group = iota((64, 128), 1) >> 4
    for upper in range(2):
        for tile in range(3):
            rows = [
                part_scr[pl.ds(tile * 1024 + upper * 8 + a, 64, stride=16), :]
                for a in range(8)
            ]
            for bit in range(3):
                low_lane = ((lane_group >> bit) & 1) == 0
                shift = 16 << bit
                for a in range(8):
                    if a & (1 << bit):
                        continue
                    first, second = rows[a], rows[a | (1 << bit)]
                    rows[a] = jnp.where(low_lane, first, pltpu.roll(second, shift, 1))
                    rows[a | (1 << bit)] = jnp.where(low_lane, pltpu.roll(first, 128 - shift, 1), second)
            for target in range(8):
                piece_scr[pl.ds(target * 6 + upper * 3 + tile, 64, stride=48), :] = rows[target]
    out_ref[...] = piece_scr[...].astype(BF16)


def contract(slot_sector, psi, left, rights):
    vmem = pl.BlockSpec(memory_space=pltpu.VMEM)
    return pl.pallas_call(
        contract_kernel,
        out_shape=jax.ShapeDtypeStruct((3072, 128), BF16),
        in_specs=[pl.BlockSpec(memory_space=pltpu.SMEM), vmem, vmem]
        + [pl.BlockSpec(memory_space=pltpu.HBM)] * 5,
        out_specs=vmem,
        scratch_shapes=[
            pltpu.VMEM((3072, 768), BF16),
            pltpu.VMEM((1024, 3072), BF16),
            pltpu.VMEM((3072, 128), F32),
            pltpu.VMEM((3072, 128), F32),
            pltpu.SemaphoreType.DMA((16,)),
        ],
        compiler_params=pltpu.CompilerParams(vmem_limit_bytes=60 << 20),
        cost_estimate=pl.CostEstimate(flops=7_000_000_000, bytes_accessed=8_000_000, transcendentals=0),
        name="contract",
    )(slot_sector, psi, left, *rights)


def collect_kernel(table_ref, piece_ref, out_ref, wide_scr):
    wide_scr[...] = piece_ref[...].astype(F32)
    slot = iota((256, 64), 0)
    chosen = ((slot >> 2) == table_ref[1:2]) & ((slot & 1) == table_ref[2:3])
    wanted = jnp.where(chosen, 1.0, 0.0).T.astype(BF16)
    for half in range(2):
        for upper in range(2):
            for tile in range(3):
                rows = wide_scr[pl.ds(half * 6 + upper * 3 + tile, 256, stride=12), :].astype(BF16)
                total = jnp.dot(wanted, rows, preferred_element_type=F32)
                first = half * 16 + upper * 8
                out_ref[first : first + 8, tile * 16 : tile * 16 + 16, :] = (
                    total.T.reshape(8, 16, 64).astype(BF16)
                )


def collect(left_table, pieces):
    vmem = pl.BlockSpec(memory_space=pltpu.VMEM)
    return pl.pallas_call(
        collect_kernel,
        out_shape=jax.ShapeDtypeStruct((32, 48, 64), BF16),
        in_specs=[vmem, vmem],
        out_specs=vmem,
        scratch_shapes=[pltpu.VMEM((3072, 128), F32)],
        compiler_params=pltpu.CompilerParams(vmem_limit_bytes=16 << 20),
        name="collect",
    )(left_table, pieces)


def pick_kernel(right_ref, out_ref):
    out_ref[...] = right_ref[:, 0]


def pick(right, term):
    return pl.pallas_call(
        pick_kernel,
        grid=(2,),
        out_shape=jax.ShapeDtypeStruct((2, 384, 384), BF16),
        in_specs=[pl.BlockSpec((1, 1, 384, 384), lambda sector: (sector, term, 0, 0))],
        out_specs=pl.BlockSpec((1, 384, 384), lambda sector: (sector, 0, 0)),
        compiler_params=pltpu.CompilerParams(vmem_limit_bytes=60 << 20),
        name="pick",
    )(right)


def per_device(psi, left, right, left_table, right_table):
    me = lax.axis_index("op")
    slot, half = (me >> 1) & 1, me & 1
    hop = lambda value, step: lax.ppermute(value, "op", [(i, (i + step) % 8) for i in range(8)])

    match = (left_table[:, 1:2] == jnp.arange(64)[None, :]) & (left_table[:, 2:3] == slot)
    source = jnp.sum(jnp.where(match, jnp.arange(64)[:, None], 0), axis=0)
    left_of = jnp.sum(jnp.where(match, left_table[:, :1], 0), axis=0)
    psi_there = lax.all_to_all(
        psi.at[source].get(mode="promise_in_bounds"), "sec", split_axis=0, concat_axis=0, tiled=True
    )

    dense = left.reshape(16, 2, 2, 16, 32).transpose(0, 3, 2, 1, 4).reshape(16, 16, 128)
    before, after, two_before, two_after = hop(dense, 1), hop(dense, -1), hop(dense, 2), hop(dense, -2)
    right_before, right_after = hop(right, 1), hop(right, -1)
    part = lambda value: jnp.where(half == 0, value[:, :, :64], value[:, :, 64:])
    table = jnp.concatenate(
        [
            jnp.concatenate([part(dense), part(before)], axis=2),
            jnp.concatenate([part(after), part(two_before)[:, :, 32:], part(two_after)[:, :, :32]], axis=2),
        ],
        axis=1,
    )
    left_here, psi_there = lax.optimization_barrier(
        (table.at[left_of].get(mode="promise_in_bounds"), psi_there)
    )
    left_there = lax.all_to_all(left_here, "sec", split_axis=0, concat_axis=0, tiled=True)
    right_two_before, right_two_after = hop(pick(right_before, 1), 1), hop(pick(right_after, 0), -1)

    slot_sector = jnp.where(slot == 0, right_table.reshape(64, 2)[:, 0], right_table.reshape(64, 2)[:, 1])
    pieces = contract(
        slot_sector,
        psi_there,
        left_there,
        [right, right_before, right_after, right_two_before, right_two_after],
    )
    pieces = lax.all_to_all(
        pieces.reshape(512, 3, 2, 128), ("sec", "op"), split_axis=0, concat_axis=0, tiled=True
    )
    return collect(left_table.T, pieces.reshape(3072, 128)).transpose(2, 0, 1)


def solution(mesh):
    in_specs = (
        P("sec", None, None),
        P("sec", "op", None, None),
        P("sec", "op", None, None),
        P("sec", None),
        P("sec"),
    )
    out_specs = P("sec", None, "op")
    return jax.shard_map(
        per_device, mesh=mesh, in_specs=in_specs, out_specs=out_specs, check_vma=False
    )
```

```python
import jax
import jax.numpy as jnp
from jax import lax
from jax.experimental import pallas as pl
from jax.experimental.pallas import tpu as pltpu
from jax.sharding import PartitionSpec as P

BF16 = jnp.bfloat16
F32 = jnp.float32


def iota(shape, dim):
    return lax.broadcasted_iota(jnp.int32, shape, dim)


def contract_kernel(sector_ref, psi_ref, left_ref, *rest):
    right_refs, (out_ref, right_scr, x_scr, part_scr, piece_scr, sem) = rest[:5], rest[5:]
    copies = []
    for term in range(8):
        for sector in range(2):
            if term < 6:
                source = right_refs[term // 2].at[sector, term % 2]
            else:
                source = right_refs[term - 3].at[sector]
            copies.append(
                pltpu.make_async_copy(
                    source,
                    right_scr.at[pl.ds(term * 384, 384), pl.ds(sector * 384, 384)],
                    sem.at[term * 2 + sector],
                )
            )
    for copy in copies:
        copy.start()

    lane, column = iota((128, 1024), 0), iota((128, 1024), 1)
    spread = jnp.where(
        ((lane >> 5) == (column >> 8)) & ((lane & 31) == (column & 31)), 1.0, 0.0
    ).astype(BF16)
    same_block = (iota((256, 256), 0) >> 5) == (iota((256, 256), 1) >> 5)

    def left_group(index, carry):
        left = left_ref[pl.ds(index * 8, 8)].reshape(256, 128)
        psi = psi_ref[pl.ds(index * 8, 8)].reshape(256, 384)
        row = pl.multiple_of(index * 128, 128)
        wide = jnp.dot(left, spread, preferred_element_type=F32)
        wide = jnp.concatenate(
            [jnp.where(same_block, wide[:, kk * 256 : kk * 256 + 256], 0.0).astype(BF16) for kk in range(4)],
            axis=0,
        )
        product = jnp.dot(wide, psi, preferred_element_type=F32).astype(BF16).reshape(4, 8, 2, 16, 384)
        for kk in range(4):
            for half in range(2):
                term = half * 4 + kk
                x_scr[pl.ds(row, 128), term * 384 : term * 384 + 384] = product[kk, :, half].reshape(128, 384)
        return carry

    lax.fori_loop(0, 8, left_group, 0, unroll=2)
    for copy in copies:
        copy.wait()

    place = iota((384, 384), 1)
    wanted = 48 * ((place >> 4) & 7) + 16 * (place >> 7) + (place & 15)
    reorder = jnp.where(iota((384, 384), 0) == wanted, 1.0, 0.0).astype(BF16)

    def right_group(index, carry):
        row = pl.multiple_of(index * 1024, 1024)
        total = jnp.dot(x_scr[pl.ds(row, 1024), :], right_scr[...], preferred_element_type=F32)
        chosen = []
        for j in range(64):
            entry = sector_ref[index * 64 + j]
            rows = total[j * 16 : j * 16 + 16]
            rows = jnp.where(entry == 1, rows[:, 384:], rows[:, :384])
            chosen.append(jnp.where(entry >= 0, rows, 0.0))
        chosen = jnp.concatenate(chosen, axis=0).astype(BF16)
        ordered = jnp.dot(chosen, reorder, preferred_element_type=F32)
        for tile in range(3):
            part_scr[pl.ds(tile * 1024 + row, 1024), :] = ordered[:, tile * 128 : tile * 128 + 128]
        return carry

    lax.fori_loop(0, 1, right_group, 0)

    lane_group = iota((64, 128), 1) >> 4
    for upper in range(2):
        for tile in range(3):
            rows = [
                part_scr[pl.ds(tile * 1024 + upper * 8 + a, 64, stride=16), :]
                for a in range(8)
            ]
            for bit in range(3):
                low_lane = ((lane_group >> bit) & 1) == 0
                shift = 16 << bit
                for a in range(8):
                    if a & (1 << bit):
                        continue
                    first, second = rows[a], rows[a | (1 << bit)]
                    rows[a] = jnp.where(low_lane, first, pltpu.roll(second, shift, 1))
                    rows[a | (1 << bit)] = jnp.where(low_lane, pltpu.roll(first, 128 - shift, 1), second)
            for target in range(8):
                piece_scr[pl.ds(target * 6 + upper * 3 + tile, 64, stride=48), :] = rows[target]
    out_ref[...] = piece_scr[...].astype(BF16)


def contract(slot_sector, psi, left, rights):
    vmem = pl.BlockSpec(memory_space=pltpu.VMEM)
    return pl.pallas_call(
        contract_kernel,
        out_shape=jax.ShapeDtypeStruct((3072, 128), BF16),
        in_specs=[pl.BlockSpec(memory_space=pltpu.SMEM), vmem, vmem]
        + [pl.BlockSpec(memory_space=pltpu.HBM)] * 5,
        out_specs=vmem,
        scratch_shapes=[
            pltpu.VMEM((3072, 768), BF16),
            pltpu.VMEM((1024, 3072), BF16),
            pltpu.VMEM((3072, 128), F32),
            pltpu.VMEM((3072, 128), F32),
            pltpu.SemaphoreType.DMA((16,)),
        ],
        compiler_params=pltpu.CompilerParams(vmem_limit_bytes=60 << 20),
        cost_estimate=pl.CostEstimate(flops=7_000_000_000, bytes_accessed=8_000_000, transcendentals=0),
        name="contract",
    )(slot_sector, psi, left, *rights)


def collect_kernel(table_ref, piece_ref, out_ref, wide_scr):
    wide_scr[...] = piece_ref[...].astype(F32)
    slot = iota((256, 64), 0)
    chosen = ((slot >> 2) == table_ref[1:2]) & ((slot & 1) == table_ref[2:3])
    wanted = jnp.where(chosen, 1.0, 0.0).T.astype(BF16)
    for half in range(2):
        for upper in range(2):
            for tile in range(3):
                rows = wide_scr[pl.ds(half * 6 + upper * 3 + tile, 256, stride=12), :].astype(BF16)
                total = jnp.dot(wanted, rows, preferred_element_type=F32)
                first = half * 16 + upper * 8
                out_ref[first : first + 8, tile * 16 : tile * 16 + 16, :] = (
                    total.T.reshape(8, 16, 64).astype(BF16)
                )


def collect(left_table, pieces):
    vmem = pl.BlockSpec(memory_space=pltpu.VMEM)
    return pl.pallas_call(
        collect_kernel,
        out_shape=jax.ShapeDtypeStruct((32, 48, 64), BF16),
        in_specs=[vmem, vmem],
        out_specs=vmem,
        scratch_shapes=[pltpu.VMEM((3072, 128), F32)],
        compiler_params=pltpu.CompilerParams(vmem_limit_bytes=16 << 20),
        name="collect",
    )(left_table, pieces)


def pick_kernel(right_ref, out_ref):
    out_ref[...] = right_ref[:, 0]


def pick(right, term):
    return pl.pallas_call(
        pick_kernel,
        grid=(2,),
        out_shape=jax.ShapeDtypeStruct((2, 384, 384), BF16),
        in_specs=[pl.BlockSpec((1, 1, 384, 384), lambda sector: (sector, term, 0, 0))],
        out_specs=pl.BlockSpec((1, 384, 384), lambda sector: (sector, 0, 0)),
        compiler_params=pltpu.CompilerParams(vmem_limit_bytes=60 << 20),
        name="pick",
    )(right)


def per_device(psi, left, right, left_table, right_table):
    me = lax.axis_index("op")
    slot, half = (me >> 1) & 1, me & 1
    hop = lambda value, step: lax.ppermute(value, "op", [(i, (i + step) % 8) for i in range(8)])

    match = (left_table[:, 1:2] == jnp.arange(64)[None, :]) & (left_table[:, 2:3] == slot)
    source = jnp.sum(jnp.where(match, jnp.arange(64)[:, None], 0), axis=0)
    left_of = jnp.sum(jnp.where(match, left_table[:, :1], 0), axis=0)
    psi_there = lax.all_to_all(
        psi.at[source].get(mode="promise_in_bounds"), "sec", split_axis=0, concat_axis=0, tiled=True
    )

    dense = left.reshape(16, 2, 2, 16, 32).transpose(0, 3, 2, 1, 4).reshape(16, 16, 128)
    two_before, two_after, again = lax.optimization_barrier((hop(dense, 2), hop(dense, -2), dense))
    before, after = hop(again, 1), hop(again, -1)
    right_before, right_after = hop(right, 1), hop(right, -1)
    part = lambda value: jnp.where(half == 0, value[:, :, :64], value[:, :, 64:])
    table = jnp.concatenate(
        [
            jnp.concatenate([part(dense), part(before)], axis=2),
            jnp.concatenate([part(after), part(two_before)[:, :, 32:], part(two_after)[:, :, :32]], axis=2),
        ],
        axis=1,
    )
    left_here, psi_there = lax.optimization_barrier(
        (table.at[left_of].get(mode="promise_in_bounds"), psi_there)
    )
    left_there = lax.all_to_all(left_here, "sec", split_axis=0, concat_axis=0, tiled=True)
    right_two_before, right_two_after = hop(pick(right_before, 1), 1), hop(pick(right_after, 0), -1)

    slot_sector = jnp.where(slot == 0, right_table.reshape(64, 2)[:, 0], right_table.reshape(64, 2)[:, 1])
    pieces = contract(
        slot_sector,
        psi_there,
        left_there,
        [right, right_before, right_after, right_two_before, right_two_after],
    )
    pieces = lax.all_to_all(
        pieces.reshape(512, 3, 2, 128), ("sec", "op"), split_axis=0, concat_axis=0, tiled=True
    )
    return collect(left_table.T, pieces.reshape(3072, 128)).transpose(2, 0, 1)


def solution(mesh):
    in_specs = (
        P("sec", None, None),
        P("sec", "op", None, None),
        P("sec", "op", None, None),
        P("sec", None),
        P("sec"),
    )
    out_specs = P("sec", None, "op")
    return jax.shard_map(
        per_device, mesh=mesh, in_specs=in_specs, out_specs=out_specs, check_vma=False
    )
```

```python
import jax
import jax.numpy as jnp
from jax import lax
from jax.experimental import pallas as pl
from jax.experimental.pallas import tpu as pltpu
from jax.sharding import PartitionSpec as P

BF16 = jnp.bfloat16
F32 = jnp.float32


def iota(shape, dim):
    return lax.broadcasted_iota(jnp.int32, shape, dim)


def right_copies(right_refs, right_scr, sem):
    copies = []
    for term, source in enumerate(right_refs):
        for sector in range(2):
            copies.append(
                pltpu.make_async_copy(
                    source(sector),
                    right_scr.at[pl.ds(term * 384, 384), pl.ds(sector * 384, 384)],
                    sem.at[term * 2 + sector],
                )
            )
    return copies


def by_sector(sector_ref, total):
    rows = []
    for j in range(64):
        here = total[j * 16 : j * 16 + 16]
        rows.append(jnp.where(sector_ref[j] == 1, here[:, 384:], here[:, :384]))
    return rows


def first_kernel(sector_ref, psi_ref, left_ref, own_ref, before_ref, after_ref, sum_ref, last_ref, right_scr, x_scr, sem):
    copies = right_copies(
        [
            lambda sector, ref=ref, term=term: ref.at[sector, term]
            for ref in (own_ref, before_ref, after_ref)
            for term in range(2)
        ],
        right_scr,
        sem,
    )
    for copy in copies:
        copy.start()

    lane, column = iota((128, 1024), 0), iota((128, 1024), 1)
    spread = jnp.where(
        ((lane >> 5) == (column >> 8)) & ((lane & 31) == (column & 31)), 1.0, 0.0
    ).astype(BF16)
    same_block = (iota((256, 256), 0) >> 5) == (iota((256, 256), 1) >> 5)

    def left_group(index, carry):
        left = left_ref[pl.ds(index * 8, 8)].reshape(256, 128)
        psi = psi_ref[pl.ds(index * 8, 8)].reshape(256, 384)
        row = pl.multiple_of(index * 128, 128)
        wide = jnp.dot(left, spread, preferred_element_type=F32)
        wide = jnp.concatenate(
            [jnp.where(same_block, wide[:, kk * 256 : kk * 256 + 256], 0.0).astype(BF16) for kk in range(4)],
            axis=0,
        )
        product = jnp.dot(wide, psi, preferred_element_type=F32).astype(BF16).reshape(4, 8, 2, 16, 384)
        for kk in range(4):
            for half in range(2):
                term = half * 4 + kk
                target, term = (x_scr, term) if term < 6 else (last_ref, term - 6)
                target[pl.ds(row, 128), term * 384 : term * 384 + 384] = product[kk, :, half].reshape(128, 384)
        return carry

    lax.fori_loop(0, 8, left_group, 0, unroll=2)
    for copy in copies:
        copy.wait()

    def right_all(index, carry):
        total = jnp.dot(x_scr[...], right_scr[...], preferred_element_type=F32)
        for j, rows in enumerate(by_sector(sector_ref, total)):
            sum_ref[j * 16 : j * 16 + 16, :] = rows
        return carry

    lax.fori_loop(0, 1, right_all, 0)


def last_kernel(sector_ref, sum_ref, last_ref, before_ref, after_ref, out_ref, right_scr, part_scr, piece_scr, sem):
    copies = right_copies([lambda sector, ref=ref: ref.at[sector] for ref in (before_ref, after_ref)], right_scr, sem)
    for copy in copies:
        copy.start()
    place = iota((384, 384), 1)
    wanted = 48 * ((place >> 4) & 7) + 16 * (place >> 7) + (place & 15)
    reorder = jnp.where(iota((384, 384), 0) == wanted, 1.0, 0.0).astype(BF16)
    for copy in copies:
        copy.wait()

    def right_all(index, carry):
        total = jnp.dot(last_ref[...], right_scr[...], preferred_element_type=F32)
        chosen = []
        for j, rows in enumerate(by_sector(sector_ref, total)):
            chosen.append(jnp.where(sector_ref[j] >= 0, rows + sum_ref[j * 16 : j * 16 + 16, :], 0.0))
        chosen = jnp.concatenate(chosen, axis=0).astype(BF16)
        ordered = jnp.dot(chosen, reorder, preferred_element_type=F32)
        for tile in range(3):
            part_scr[pl.ds(tile * 1024, 1024), :] = ordered[:, tile * 128 : tile * 128 + 128]
        return carry

    lax.fori_loop(0, 1, right_all, 0)

    lane_group = iota((64, 128), 1) >> 4
    for upper in range(2):
        for tile in range(3):
            rows = [
                part_scr[pl.ds(tile * 1024 + upper * 8 + a, 64, stride=16), :]
                for a in range(8)
            ]
            for bit in range(3):
                low_lane = ((lane_group >> bit) & 1) == 0
                shift = 16 << bit
                for a in range(8):
                    if a & (1 << bit):
                        continue
                    first, second = rows[a], rows[a | (1 << bit)]
                    rows[a] = jnp.where(low_lane, first, pltpu.roll(second, shift, 1))
                    rows[a | (1 << bit)] = jnp.where(low_lane, pltpu.roll(first, 128 - shift, 1), second)
            for target in range(8):
                piece_scr[pl.ds(target * 6 + upper * 3 + tile, 64, stride=48), :] = rows[target]
    out_ref[...] = piece_scr[...].astype(BF16)


def contract(slot_sector, psi, left, rights):
    vmem = pl.BlockSpec(memory_space=pltpu.VMEM)
    hbm = pl.BlockSpec(memory_space=pltpu.HBM)
    smem = pl.BlockSpec(memory_space=pltpu.SMEM)
    sums, last = pl.pallas_call(
        first_kernel,
        out_shape=[jax.ShapeDtypeStruct((1024, 384), F32), jax.ShapeDtypeStruct((1024, 768), BF16)],
        in_specs=[smem, vmem, vmem, hbm, hbm, hbm],
        out_specs=[vmem, vmem],
        scratch_shapes=[
            pltpu.VMEM((2304, 768), BF16),
            pltpu.VMEM((1024, 2304), BF16),
            pltpu.SemaphoreType.DMA((12,)),
        ],
        compiler_params=pltpu.CompilerParams(vmem_limit_bytes=60 << 20),
        cost_estimate=pl.CostEstimate(flops=6_000_000_000, bytes_accessed=9_000_000, transcendentals=0),
        name="contract_first",
    )(slot_sector, psi, left, *rights[:3])
    return pl.pallas_call(
        last_kernel,
        out_shape=jax.ShapeDtypeStruct((3072, 128), BF16),
        in_specs=[smem, vmem, vmem, hbm, hbm],
        out_specs=vmem,
        scratch_shapes=[
            pltpu.VMEM((768, 768), BF16),
            pltpu.VMEM((3072, 128), F32),
            pltpu.VMEM((3072, 128), F32),
            pltpu.SemaphoreType.DMA((4,)),
        ],
        compiler_params=pltpu.CompilerParams(vmem_limit_bytes=60 << 20),
        cost_estimate=pl.CostEstimate(flops=2_000_000_000, bytes_accessed=5_000_000, transcendentals=0),
        name="contract_last",
    )(slot_sector, sums, last, *rights[3:])


def collect_kernel(table_ref, piece_ref, out_ref, wide_scr):
    wide_scr[...] = piece_ref[...].astype(F32)
    slot = iota((256, 64), 0)
    chosen = ((slot >> 2) == table_ref[1:2]) & ((slot & 1) == table_ref[2:3])
    wanted = jnp.where(chosen, 1.0, 0.0).T.astype(BF16)
    for half in range(2):
        for upper in range(2):
            for tile in range(3):
                rows = wide_scr[pl.ds(half * 6 + upper * 3 + tile, 256, stride=12), :].astype(BF16)
                total = jnp.dot(wanted, rows, preferred_element_type=F32)
                first = half * 16 + upper * 8
                out_ref[first : first + 8, tile * 16 : tile * 16 + 16, :] = (
                    total.T.reshape(8, 16, 64).astype(BF16)
                )


def collect(left_table, pieces):
    vmem = pl.BlockSpec(memory_space=pltpu.VMEM)
    return pl.pallas_call(
        collect_kernel,
        out_shape=jax.ShapeDtypeStruct((32, 48, 64), BF16),
        in_specs=[vmem, vmem],
        out_specs=vmem,
        scratch_shapes=[pltpu.VMEM((3072, 128), F32)],
        compiler_params=pltpu.CompilerParams(vmem_limit_bytes=16 << 20),
        name="collect",
    )(left_table, pieces)


def pick_kernel(right_ref, out_ref):
    out_ref[...] = right_ref[:, 0]


def pick(right, term):
    return pl.pallas_call(
        pick_kernel,
        grid=(2,),
        out_shape=jax.ShapeDtypeStruct((2, 384, 384), BF16),
        in_specs=[pl.BlockSpec((1, 1, 384, 384), lambda sector: (sector, term, 0, 0))],
        out_specs=pl.BlockSpec((1, 384, 384), lambda sector: (sector, 0, 0)),
        compiler_params=pltpu.CompilerParams(vmem_limit_bytes=60 << 20),
        name="pick",
    )(right)


def per_device(psi, left, right, left_table, right_table):
    me = lax.axis_index("op")
    slot, half = (me >> 1) & 1, me & 1
    hop = lambda value, step: lax.ppermute(value, "op", [(i, (i + step) % 8) for i in range(8)])

    match = (left_table[:, 1:2] == jnp.arange(64)[None, :]) & (left_table[:, 2:3] == slot)
    source = jnp.sum(jnp.where(match, jnp.arange(64)[:, None], 0), axis=0)
    left_of = jnp.sum(jnp.where(match, left_table[:, :1], 0), axis=0)
    psi_there = lax.all_to_all(
        psi.at[source].get(mode="promise_in_bounds"), "sec", split_axis=0, concat_axis=0, tiled=True
    )

    dense = left.reshape(16, 2, 2, 16, 32).transpose(0, 3, 2, 1, 4).reshape(16, 16, 128)
    before, after, two_before, two_after = hop(dense, 1), hop(dense, -1), hop(dense, 2), hop(dense, -2)
    right_before, right_after = hop(right, 1), hop(right, -1)
    part = lambda value: jnp.where(half == 0, value[:, :, :64], value[:, :, 64:])
    table = jnp.concatenate(
        [
            jnp.concatenate([part(dense), part(before)], axis=2),
            jnp.concatenate([part(after), part(two_before)[:, :, 32:], part(two_after)[:, :, :32]], axis=2),
        ],
        axis=1,
    )
    left_here, psi_there = lax.optimization_barrier(
        (table.at[left_of].get(mode="promise_in_bounds"), psi_there)
    )
    left_there = lax.all_to_all(left_here, "sec", split_axis=0, concat_axis=0, tiled=True)
    right_two_before, right_two_after = hop(pick(right_before, 1), 1), hop(pick(right_after, 0), -1)

    slot_sector = jnp.where(slot == 0, right_table.reshape(64, 2)[:, 0], right_table.reshape(64, 2)[:, 1])
    pieces = contract(
        slot_sector,
        psi_there,
        left_there,
        [right, right_before, right_after, right_two_before, right_two_after],
    )
    pieces = lax.all_to_all(
        pieces.reshape(512, 3, 2, 128), ("sec", "op"), split_axis=0, concat_axis=0, tiled=True
    )
    return collect(left_table.T, pieces.reshape(3072, 128)).transpose(2, 0, 1)


def solution(mesh):
    in_specs = (
        P("sec", None, None),
        P("sec", "op", None, None),
        P("sec", "op", None, None),
        P("sec", None),
        P("sec"),
    )
    out_specs = P("sec", None, "op")
    return jax.shard_map(
        per_device, mesh=mesh, in_specs=in_specs, out_specs=out_specs, check_vma=False
    )
```

```python
import jax
import jax.numpy as jnp
from jax import lax
from jax.experimental import pallas as pl
from jax.experimental.pallas import tpu as pltpu
from jax.sharding import PartitionSpec as P

BF16 = jnp.bfloat16
F32 = jnp.float32


def iota(shape, dim):
    return lax.broadcasted_iota(jnp.int32, shape, dim)


def right_copies(right_refs, right_scr, sem):
    copies = []
    for term, source in enumerate(right_refs):
        for sector in range(2):
            copies.append(
                pltpu.make_async_copy(
                    source(sector),
                    right_scr.at[pl.ds(term * 384, 384), pl.ds(sector * 384, 384)],
                    sem.at[term * 2 + sector],
                )
            )
    return copies


def by_sector(sector_ref, total):
    rows = []
    for j in range(64):
        here = total[j * 16 : j * 16 + 16]
        rows.append(jnp.where(sector_ref[j] == 1, here[:, 384:], here[:, :384]))
    return rows


def first_kernel(sector_ref, psi_ref, left_ref, own_ref, before_ref, after_ref, sum_ref, last_ref, right_scr, x_scr, sem):
    copies = right_copies(
        [
            lambda sector, ref=ref, term=term: ref.at[sector, term]
            for ref in (own_ref, before_ref, after_ref)
            for term in range(2)
        ],
        right_scr,
        sem,
    )
    for copy in copies:
        copy.start()

    lane, column = iota((128, 1024), 0), iota((128, 1024), 1)
    spread = jnp.where(
        ((lane >> 5) == (column >> 8)) & ((lane & 31) == (column & 31)), 1.0, 0.0
    ).astype(BF16)
    same_block = (iota((256, 256), 0) >> 5) == (iota((256, 256), 1) >> 5)

    def left_group(index, carry):
        left = left_ref[pl.ds(index * 8, 8)].reshape(256, 128)
        psi = psi_ref[pl.ds(index * 8, 8)].reshape(256, 384)
        row = pl.multiple_of(index * 128, 128)
        wide = jnp.dot(left, spread, preferred_element_type=F32)
        wide = jnp.concatenate(
            [jnp.where(same_block, wide[:, kk * 256 : kk * 256 + 256], 0.0).astype(BF16) for kk in range(4)],
            axis=0,
        )
        product = jnp.dot(wide, psi, preferred_element_type=F32).astype(BF16).reshape(4, 8, 2, 16, 384)
        for kk in range(4):
            for half in range(2):
                term = half * 4 + kk
                target, term = (x_scr, term) if term < 6 else (last_ref, term - 6)
                target[pl.ds(row, 128), term * 384 : term * 384 + 384] = product[kk, :, half].reshape(128, 384)
        return carry

    lax.fori_loop(0, 8, left_group, 0, unroll=2)
    for copy in copies:
        copy.wait()

    def right_all(index, carry):
        total = jnp.dot(x_scr[...], right_scr[...], preferred_element_type=F32)
        for j, rows in enumerate(by_sector(sector_ref, total)):
            sum_ref[j * 16 : j * 16 + 16, :] = rows
        return carry

    lax.fori_loop(0, 1, right_all, 0)


def last_kernel(sector_ref, sum_ref, last_ref, before_ref, after_ref, out_ref, right_scr, part_scr, piece_scr, sem):
    copies = right_copies([lambda sector, ref=ref: ref.at[sector] for ref in (before_ref, after_ref)], right_scr, sem)
    for copy in copies:
        copy.start()
    place = iota((384, 384), 1)
    wanted = 48 * ((place >> 4) & 7) + 16 * (place >> 7) + (place & 15)
    reorder = jnp.where(iota((384, 384), 0) == wanted, 1.0, 0.0).astype(BF16)
    for copy in copies:
        copy.wait()

    def right_all(index, carry):
        total = jnp.dot(last_ref[...], right_scr[...], preferred_element_type=F32)
        chosen = []
        for j, rows in enumerate(by_sector(sector_ref, total)):
            chosen.append(jnp.where(sector_ref[j] >= 0, rows + sum_ref[j * 16 : j * 16 + 16, :], 0.0))
        chosen = jnp.concatenate(chosen, axis=0).astype(BF16)
        ordered = jnp.dot(chosen, reorder, preferred_element_type=F32)
        for tile in range(3):
            part_scr[pl.ds(tile * 1024, 1024), :] = ordered[:, tile * 128 : tile * 128 + 128]
        return carry

    lax.fori_loop(0, 1, right_all, 0)

    lane_group = iota((64, 128), 1) >> 4
    for upper in range(2):
        for tile in range(3):
            rows = [
                part_scr[pl.ds(tile * 1024 + upper * 8 + a, 64, stride=16), :]
                for a in range(8)
            ]
            for bit in range(3):
                low_lane = ((lane_group >> bit) & 1) == 0
                shift = 16 << bit
                for a in range(8):
                    if a & (1 << bit):
                        continue
                    first, second = rows[a], rows[a | (1 << bit)]
                    rows[a] = jnp.where(low_lane, first, pltpu.roll(second, shift, 1))
                    rows[a | (1 << bit)] = jnp.where(low_lane, pltpu.roll(first, 128 - shift, 1), second)
            for target in range(8):
                piece_scr[pl.ds(target * 6 + upper * 3 + tile, 64, stride=48), :] = rows[target]
    out_ref[...] = piece_scr[...].astype(BF16)


def contract(slot_sector, psi, left, rights):
    rights = [pltpu.with_memory_space_constraint(value, pltpu.HBM) for value in rights]
    vmem = pl.BlockSpec(memory_space=pltpu.VMEM)
    hbm = pl.BlockSpec(memory_space=pltpu.HBM)
    smem = pl.BlockSpec(memory_space=pltpu.SMEM)
    sums, last = pl.pallas_call(
        first_kernel,
        out_shape=[jax.ShapeDtypeStruct((1024, 384), F32), jax.ShapeDtypeStruct((1024, 768), BF16)],
        in_specs=[smem, vmem, vmem, hbm, hbm, hbm],
        out_specs=[vmem, vmem],
        scratch_shapes=[
            pltpu.VMEM((2304, 768), BF16),
            pltpu.VMEM((1024, 2304), BF16),
            pltpu.SemaphoreType.DMA((12,)),
        ],
        compiler_params=pltpu.CompilerParams(vmem_limit_bytes=28 << 20),
        cost_estimate=pl.CostEstimate(flops=6_000_000_000, bytes_accessed=9_000_000, transcendentals=0),
        name="contract_first",
    )(slot_sector, psi, left, *rights[:3])
    return pl.pallas_call(
        last_kernel,
        out_shape=jax.ShapeDtypeStruct((3072, 128), BF16),
        in_specs=[smem, vmem, vmem, hbm, hbm],
        out_specs=vmem,
        scratch_shapes=[
            pltpu.VMEM((768, 768), BF16),
            pltpu.VMEM((3072, 128), F32),
            pltpu.VMEM((3072, 128), F32),
            pltpu.SemaphoreType.DMA((4,)),
        ],
        compiler_params=pltpu.CompilerParams(vmem_limit_bytes=20 << 20),
        cost_estimate=pl.CostEstimate(flops=2_000_000_000, bytes_accessed=5_000_000, transcendentals=0),
        name="contract_last",
    )(slot_sector, sums, last, *rights[3:])


def collect_kernel(table_ref, piece_ref, out_ref, wide_scr):
    wide_scr[...] = piece_ref[...].astype(F32)
    slot = iota((256, 64), 0)
    chosen = ((slot >> 2) == table_ref[1:2]) & ((slot & 1) == table_ref[2:3])
    wanted = jnp.where(chosen, 1.0, 0.0).T.astype(BF16)
    for half in range(2):
        for upper in range(2):
            for tile in range(3):
                rows = wide_scr[pl.ds(half * 6 + upper * 3 + tile, 256, stride=12), :].astype(BF16)
                total = jnp.dot(wanted, rows, preferred_element_type=F32)
                first = half * 16 + upper * 8
                out_ref[first : first + 8, tile * 16 : tile * 16 + 16, :] = (
                    total.T.reshape(8, 16, 64).astype(BF16)
                )


def collect(left_table, pieces):
    vmem = pl.BlockSpec(memory_space=pltpu.VMEM)
    return pl.pallas_call(
        collect_kernel,
        out_shape=jax.ShapeDtypeStruct((32, 48, 64), BF16),
        in_specs=[vmem, vmem],
        out_specs=vmem,
        scratch_shapes=[pltpu.VMEM((3072, 128), F32)],
        compiler_params=pltpu.CompilerParams(vmem_limit_bytes=16 << 20),
        name="collect",
    )(left_table, pieces)


def pick_kernel(right_ref, out_ref):
    out_ref[...] = right_ref[:, 0]


def pick(right, term):
    return pl.pallas_call(
        pick_kernel,
        grid=(2,),
        out_shape=jax.ShapeDtypeStruct((2, 384, 384), BF16),
        in_specs=[pl.BlockSpec((1, 1, 384, 384), lambda sector: (sector, term, 0, 0))],
        out_specs=pl.BlockSpec((1, 384, 384), lambda sector: (sector, 0, 0)),
        compiler_params=pltpu.CompilerParams(vmem_limit_bytes=60 << 20),
        name="pick",
    )(right)


def per_device(psi, left, right, left_table, right_table):
    me = lax.axis_index("op")
    slot, half = (me >> 1) & 1, me & 1
    hop = lambda value, step: lax.ppermute(value, "op", [(i, (i + step) % 8) for i in range(8)])

    match = (left_table[:, 1:2] == jnp.arange(64)[None, :]) & (left_table[:, 2:3] == slot)
    source = jnp.sum(jnp.where(match, jnp.arange(64)[:, None], 0), axis=0)
    left_of = jnp.sum(jnp.where(match, left_table[:, :1], 0), axis=0)
    psi_there = lax.all_to_all(
        psi.at[source].get(mode="promise_in_bounds"), "sec", split_axis=0, concat_axis=0, tiled=True
    )

    dense = left.reshape(16, 2, 2, 16, 32).transpose(0, 3, 2, 1, 4).reshape(16, 16, 128)
    before, after, two_before, two_after = hop(dense, 1), hop(dense, -1), hop(dense, 2), hop(dense, -2)
    right_before, right_after = hop(right, 1), hop(right, -1)
    part = lambda value: jnp.where(half == 0, value[:, :, :64], value[:, :, 64:])
    table = jnp.concatenate(
        [
            jnp.concatenate([part(dense), part(before)], axis=2),
            jnp.concatenate([part(after), part(two_before)[:, :, 32:], part(two_after)[:, :, :32]], axis=2),
        ],
        axis=1,
    )
    left_here, psi_there = lax.optimization_barrier(
        (table.at[left_of].get(mode="promise_in_bounds"), psi_there)
    )
    left_there = lax.all_to_all(left_here, "sec", split_axis=0, concat_axis=0, tiled=True)
    right_two_before, right_two_after = hop(pick(right_before, 1), 1), hop(pick(right_after, 0), -1)

    slot_sector = jnp.where(slot == 0, right_table.reshape(64, 2)[:, 0], right_table.reshape(64, 2)[:, 1])
    pieces = contract(
        slot_sector,
        psi_there,
        left_there,
        [right, right_before, right_after, right_two_before, right_two_after],
    )
    pieces = lax.all_to_all(
        pieces.reshape(512, 3, 2, 128), ("sec", "op"), split_axis=0, concat_axis=0, tiled=True
    )
    return collect(left_table.T, pieces.reshape(3072, 128)).transpose(2, 0, 1)


def solution(mesh):
    in_specs = (
        P("sec", None, None),
        P("sec", "op", None, None),
        P("sec", "op", None, None),
        P("sec", None),
        P("sec"),
    )
    out_specs = P("sec", None, "op")
    return jax.shard_map(
        per_device, mesh=mesh, in_specs=in_specs, out_specs=out_specs, check_vma=False
    )
```

```python
import jax
import jax.numpy as jnp
from jax import lax
from jax.experimental import pallas as pl
from jax.experimental.pallas import tpu as pltpu
from jax.sharding import PartitionSpec as P

BF16 = jnp.bfloat16
F32 = jnp.float32


def iota(shape, dim):
    return lax.broadcasted_iota(jnp.int32, shape, dim)


def right_copies(right_refs, right_scr, sem):
    copies = []
    for term, source in enumerate(right_refs):
        for sector in range(2):
            copies.append(
                pltpu.make_async_copy(
                    source(sector),
                    right_scr.at[pl.ds(term * 384, 384), pl.ds(sector * 384, 384)],
                    sem.at[term * 2 + sector],
                )
            )
    return copies


def by_sector(sector_ref, total):
    rows = []
    for j in range(64):
        here = total[j * 16 : j * 16 + 16]
        rows.append(jnp.where(sector_ref[j] == 1, here[:, 384:], here[:, :384]))
    return rows


def first_kernel(sector_ref, psi_ref, left_ref, own_ref, before_ref, after_ref, sum_ref, last_ref, right_scr, x_scr, sem):
    copies = right_copies(
        [
            lambda sector, ref=ref, term=term: ref.at[sector, term]
            for ref in (own_ref, before_ref, after_ref)
            for term in range(2)
        ],
        right_scr,
        sem,
    )
    for copy in copies:
        copy.start()

    lane, column = iota((128, 1024), 0), iota((128, 1024), 1)
    spread = jnp.where(
        ((lane >> 5) == (column >> 8)) & ((lane & 31) == (column & 31)), 1.0, 0.0
    ).astype(BF16)
    same_block = (iota((256, 256), 0) >> 5) == (iota((256, 256), 1) >> 5)

    def left_group(index, carry):
        left = left_ref[pl.ds(index * 8, 8)].reshape(256, 128)
        psi = psi_ref[pl.ds(index * 8, 8)].reshape(256, 384)
        row = pl.multiple_of(index * 128, 128)
        wide = jnp.dot(left, spread, preferred_element_type=F32)
        wide = jnp.concatenate(
            [jnp.where(same_block, wide[:, kk * 256 : kk * 256 + 256], 0.0).astype(BF16) for kk in range(4)],
            axis=0,
        )
        product = jnp.dot(wide, psi, preferred_element_type=F32).astype(BF16).reshape(4, 8, 2, 16, 384)
        for kk in range(4):
            for half in range(2):
                term = half * 4 + kk
                target, term = (x_scr, term) if term < 6 else (last_ref, term - 6)
                target[pl.ds(row, 128), term * 384 : term * 384 + 384] = product[kk, :, half].reshape(128, 384)
        return carry

    lax.fori_loop(0, 8, left_group, 0, unroll=4)
    for copy in copies:
        copy.wait()

    def right_all(index, carry):
        total = jnp.dot(x_scr[...], right_scr[...], preferred_element_type=F32)
        for j, rows in enumerate(by_sector(sector_ref, total)):
            sum_ref[j * 16 : j * 16 + 16, :] = rows
        return carry

    lax.fori_loop(0, 1, right_all, 0)


def last_kernel(sector_ref, sum_ref, last_ref, before_ref, after_ref, out_ref, right_scr, part_scr, piece_scr, sem):
    copies = right_copies([lambda sector, ref=ref: ref.at[sector] for ref in (before_ref, after_ref)], right_scr, sem)
    for copy in copies:
        copy.start()
    place = iota((384, 384), 1)
    wanted = 48 * ((place >> 4) & 7) + 16 * (place >> 7) + (place & 15)
    reorder = jnp.where(iota((384, 384), 0) == wanted, 1.0, 0.0).astype(BF16)
    for copy in copies:
        copy.wait()

    def right_all(index, carry):
        total = jnp.dot(last_ref[...], right_scr[...], preferred_element_type=F32)
        chosen = []
        for j, rows in enumerate(by_sector(sector_ref, total)):
            chosen.append(jnp.where(sector_ref[j] >= 0, rows + sum_ref[j * 16 : j * 16 + 16, :], 0.0))
        chosen = jnp.concatenate(chosen, axis=0).astype(BF16)
        ordered = jnp.dot(chosen, reorder, preferred_element_type=F32)
        for tile in range(3):
            part_scr[pl.ds(tile * 1024, 1024), :] = ordered[:, tile * 128 : tile * 128 + 128]
        return carry

    lax.fori_loop(0, 1, right_all, 0)

    lane_group = iota((64, 128), 1) >> 4
    for upper in range(2):
        for tile in range(3):
            rows = [
                part_scr[pl.ds(tile * 1024 + upper * 8 + a, 64, stride=16), :]
                for a in range(8)
            ]
            for bit in range(3):
                low_lane = ((lane_group >> bit) & 1) == 0
                shift = 16 << bit
                for a in range(8):
                    if a & (1 << bit):
                        continue
                    first, second = rows[a], rows[a | (1 << bit)]
                    rows[a] = jnp.where(low_lane, first, pltpu.roll(second, shift, 1))
                    rows[a | (1 << bit)] = jnp.where(low_lane, pltpu.roll(first, 128 - shift, 1), second)
            for target in range(8):
                piece_scr[pl.ds(target * 6 + upper * 3 + tile, 64, stride=48), :] = rows[target]
    out_ref[...] = piece_scr[...].astype(BF16)


def contract(slot_sector, psi, left, rights):
    rights = [pltpu.with_memory_space_constraint(value, pltpu.HBM) for value in rights]
    vmem = pl.BlockSpec(memory_space=pltpu.VMEM)
    hbm = pl.BlockSpec(memory_space=pltpu.HBM)
    smem = pl.BlockSpec(memory_space=pltpu.SMEM)
    sums, last = pl.pallas_call(
        first_kernel,
        out_shape=[jax.ShapeDtypeStruct((1024, 384), F32), jax.ShapeDtypeStruct((1024, 768), BF16)],
        in_specs=[smem, vmem, vmem, hbm, hbm, hbm],
        out_specs=[vmem, vmem],
        scratch_shapes=[
            pltpu.VMEM((2304, 768), BF16),
            pltpu.VMEM((1024, 2304), BF16),
            pltpu.SemaphoreType.DMA((12,)),
        ],
        compiler_params=pltpu.CompilerParams(vmem_limit_bytes=28 << 20),
        cost_estimate=pl.CostEstimate(flops=6_000_000_000, bytes_accessed=9_000_000, transcendentals=0),
        name="contract_first",
    )(slot_sector, psi, left, *rights[:3])
    return pl.pallas_call(
        last_kernel,
        out_shape=jax.ShapeDtypeStruct((3072, 128), BF16),
        in_specs=[smem, vmem, vmem, hbm, hbm],
        out_specs=vmem,
        scratch_shapes=[
            pltpu.VMEM((768, 768), BF16),
            pltpu.VMEM((3072, 128), F32),
            pltpu.VMEM((3072, 128), F32),
            pltpu.SemaphoreType.DMA((4,)),
        ],
        compiler_params=pltpu.CompilerParams(vmem_limit_bytes=20 << 20),
        cost_estimate=pl.CostEstimate(flops=2_000_000_000, bytes_accessed=5_000_000, transcendentals=0),
        name="contract_last",
    )(slot_sector, sums, last, *rights[3:])


def collect_kernel(table_ref, piece_ref, out_ref, wide_scr):
    wide_scr[...] = piece_ref[...].astype(F32)
    slot = iota((256, 64), 0)
    chosen = ((slot >> 2) == table_ref[1:2]) & ((slot & 1) == table_ref[2:3])
    wanted = jnp.where(chosen, 1.0, 0.0).T.astype(BF16)
    for half in range(2):
        for upper in range(2):
            for tile in range(3):
                rows = wide_scr[pl.ds(half * 6 + upper * 3 + tile, 256, stride=12), :].astype(BF16)
                total = jnp.dot(wanted, rows, preferred_element_type=F32)
                first = half * 16 + upper * 8
                out_ref[first : first + 8, tile * 16 : tile * 16 + 16, :] = (
                    total.T.reshape(8, 16, 64).astype(BF16)
                )


def collect(left_table, pieces):
    vmem = pl.BlockSpec(memory_space=pltpu.VMEM)
    return pl.pallas_call(
        collect_kernel,
        out_shape=jax.ShapeDtypeStruct((32, 48, 64), BF16),
        in_specs=[vmem, vmem],
        out_specs=vmem,
        scratch_shapes=[pltpu.VMEM((3072, 128), F32)],
        compiler_params=pltpu.CompilerParams(vmem_limit_bytes=16 << 20),
        name="collect",
    )(left_table, pieces)


def pick_kernel(right_ref, out_ref):
    out_ref[...] = right_ref[:, 0]


def pick(right, term):
    return pl.pallas_call(
        pick_kernel,
        grid=(2,),
        out_shape=jax.ShapeDtypeStruct((2, 384, 384), BF16),
        in_specs=[pl.BlockSpec((1, 1, 384, 384), lambda sector: (sector, term, 0, 0))],
        out_specs=pl.BlockSpec((1, 384, 384), lambda sector: (sector, 0, 0)),
        compiler_params=pltpu.CompilerParams(vmem_limit_bytes=60 << 20),
        name="pick",
    )(right)


def route_kernel(table_ref, slot_ref, psi_ref, out_ref, left_ref, source_ref):
    def clear(owner, carry):
        source_ref[owner] = 0
        left_ref[owner] = 0
        return carry

    def enter(block, carry):
        @pl.when(table_ref[2, block] == slot_ref[0])
        def _():
            owner = table_ref[1, block]
            source_ref[owner] = block
            left_ref[owner] = table_ref[0, block]

        return carry

    def move(owner, carry):
        out_ref[owner] = psi_ref[source_ref[owner]]
        return carry

    lax.fori_loop(0, 64, clear, 0, unroll=8)
    lax.fori_loop(0, 64, enter, 0, unroll=8)
    lax.fori_loop(0, 64, move, 0, unroll=4)


def route(table, slot, psi):
    vmem = pl.BlockSpec(memory_space=pltpu.VMEM)
    smem = pl.BlockSpec(memory_space=pltpu.SMEM)
    return pl.pallas_call(
        route_kernel,
        out_shape=[jax.ShapeDtypeStruct((64, 32, 384), BF16), jax.ShapeDtypeStruct((64,), jnp.int32)],
        in_specs=[smem, smem, vmem],
        out_specs=[vmem, smem],
        scratch_shapes=[pltpu.SMEM((64,), jnp.int32)],
        compiler_params=pltpu.CompilerParams(vmem_limit_bytes=8 << 20),
        name="route",
    )(table, slot, psi)


def per_device(psi, left, right, left_table, right_table):
    me = lax.axis_index("op")
    slot, half = (me >> 1) & 1, me & 1
    hop = lambda value, step: lax.ppermute(value, "op", [(i, (i + step) % 8) for i in range(8)])

    psi_here, left_of = route(left_table.T, slot.reshape(1), psi)
    psi_there = lax.all_to_all(psi_here, "sec", split_axis=0, concat_axis=0, tiled=True)

    dense = left.reshape(16, 2, 2, 16, 32).transpose(0, 3, 2, 1, 4).reshape(16, 16, 128)
    before, after, two_before, two_after = hop(dense, 1), hop(dense, -1), hop(dense, 2), hop(dense, -2)
    right_before, right_after = hop(right, 1), hop(right, -1)
    part = lambda value: jnp.where(half == 0, value[:, :, :64], value[:, :, 64:])
    table = jnp.concatenate(
        [
            jnp.concatenate([part(dense), part(before)], axis=2),
            jnp.concatenate([part(after), part(two_before)[:, :, 32:], part(two_after)[:, :, :32]], axis=2),
        ],
        axis=1,
    )
    left_here, psi_there = lax.optimization_barrier(
        (table.at[left_of].get(mode="promise_in_bounds"), psi_there)
    )
    left_there = lax.all_to_all(left_here, "sec", split_axis=0, concat_axis=0, tiled=True)
    right_two_before, right_two_after = hop(pick(right_before, 1), 1), hop(pick(right_after, 0), -1)

    slot_sector = jnp.where(slot == 0, right_table.reshape(64, 2)[:, 0], right_table.reshape(64, 2)[:, 1])
    pieces = contract(
        slot_sector,
        psi_there,
        left_there,
        [right, right_before, right_after, right_two_before, right_two_after],
    )
    pieces = lax.all_to_all(
        pieces.reshape(512, 3, 2, 128), ("sec", "op"), split_axis=0, concat_axis=0, tiled=True
    )
    return collect(left_table.T, pieces.reshape(3072, 128)).transpose(2, 0, 1)


def solution(mesh):
    in_specs = (
        P("sec", None, None),
        P("sec", "op", None, None),
        P("sec", "op", None, None),
        P("sec", None),
        P("sec"),
    )
    out_specs = P("sec", None, "op")
    return jax.shard_map(
        per_device, mesh=mesh, in_specs=in_specs, out_specs=out_specs, check_vma=False
    )
```
